128 devices in a mesh: width: 8 (over z_lo, x), seq: 16 (over z_hi, y, core).
Axes of the slice: x: 4, y: 4, z: 4 (z_hi: 2, z_lo: 2; z = z_hi * 2 + z_lo), core: 2. Of those that a mesh axis runs over, the one named last changes fastest.
Arguments:
- activations: bfloat16 [16384, 28672], P('seq', 'width'), may hold values from -6 to 6
- errors: bfloat16 [16384, 8192], P('seq', 'width'), may hold values from -6 to 6
- proj_acts: bfloat16 [28672, 128], P('width'), may hold values from -0.03125 to 0.03125
- proj_errs: bfloat16 [8192, 128], P('width'), may hold values from -0.0625 to 0.0625
- fisher: float32 [16384, 16384], P('seq', 'width'), may hold values from -1 to 4, as said below
- queries: float32 [16, 1024, 128], P('seq', 'width'), may hold values from -6 to 6
Outputs:
- solution: float32 [16, 1024, 128], P('seq', 'width')
- residual: float32 [16, 1024, 128], P('seq', 'width')
- scores: float32 [256, 128], P(('width', 'seq'))
The draws below stay inside these ranges and needn't reach their ends.
Inputs may be any that keep to these rules, and one draw needn't show every extreme that they name: `fisher`: symmetric and positive definite.
All inputs are finite; a program needn't handle non-finite values.
Results may differ from the reference program's by a relative error of at most 0.003.
Values may be sent and summed in bfloat16 or wider, within the bound.
A program may use at most 128 MiB of HBM per device.

```python
import math
import jax
import jax.numpy as jnp
from jax import lax

DA = 28672
DG = 8192
RANK = 128
SEQ_LEN = 64
QUERIES = 128
SEQS = 256
TOKENS = 16384
ENTRIES = 16384
N_SEQ = 16


def draw_fisher(key, part):
    key_diag = jax.random.fold_in(key, 11)
    key_off = jax.random.fold_in(key, 23)
    order = ENTRIES
    diag_values = jax.random.uniform(key_diag, (order,), jnp.float32, 2.0, 3.0)
    spread = jnp.clip(jax.random.normal(key_off, (order, order), jnp.float32), -6.0, 6.0)
    symmetric = (spread + spread.T) * (0.6 / (math.sqrt(2.0) * math.sqrt(order)))
    diag_index = jnp.arange(order)
    return symmetric.at[diag_index, diag_index].add(diag_values)


def steps_of(stream_key, shape, pieces, smallest, high):
    loudness, own = 1.0, jax.random.fold_in(stream_key, 6)
    for dim, parts in pieces:
        draws = jnp.exp(jax.random.uniform(jax.random.fold_in(own, dim), (parts,), jnp.float32, smallest / len(pieces), high / len(pieces)))
        loudness = loudness * jnp.repeat(draws, shape[dim] // parts).reshape([-1 if axis == dim else 1 for axis in range(len(shape))])
    return loudness


def normal_values(key, extent, scale, reach, split=(), held_as=jnp.bfloat16):
    entries = scale * jax.random.normal(key, extent, jnp.float32)
    if split:
        entries = entries * steps_of(key, extent, split, -0.22, 0.18)
    return jnp.clip(entries, -reach, reach).astype(held_as)


def setup_inputs(seed: int = 0) -> dict:
    keys = jax.random.split(jax.random.key(seed), 7)
    return {
        "activations": normal_values(keys[0], (TOKENS, DA), 1.0, 6.0, ((0, 16), (1, 8))),
        "errors": normal_values(keys[1], (TOKENS, DG), 1.0, 6.0, ((0, 16), (1, 8))),
        "proj_acts": normal_values(keys[2], (DA, RANK), DA ** -0.5, 0.03125, ((0, 8),)),
        "proj_errs": normal_values(keys[3], (DG, RANK), DG ** -0.5, 0.0625, ((0, 8),)),
        "fisher": draw_fisher(jax.random.fold_in(keys[6], 71), 0),
        "queries": normal_values(keys[5], (N_SEQ, ENTRIES // N_SEQ, QUERIES), 1.0, 6.0, ((0, 16), (1, 8)), jnp.float32),
    }


ridge_damp = 0.1
bound_low = 0.5
bound_high = 6.0


def chebyshev(apply_op, rhs):
    center = 0.5 * (bound_high + bound_low)
    half_width = 0.5 * (bound_high - bound_low)
    sigma_ratio = center / half_width
    rho_first = 1.0 / sigma_ratio
    rho_second = 1.0 / (2.0 * sigma_ratio - rho_first)
    step_one = rhs / center
    residue = rhs - apply_op(step_one)
    step_two = (rho_second * rho_first) * step_one + (2.0 * rho_second / half_width) * residue
    iterate = step_one + step_two
    residue = residue - apply_op(step_two)
    return iterate, residue


def reference(activations, errors, proj_acts, proj_errs, fisher, queries):
    highest = lax.Precision.HIGHEST
    act_proj = jnp.dot(activations, proj_acts, preferred_element_type=jnp.float32).reshape(SEQS, SEQ_LEN, RANK)
    err_proj = jnp.dot(errors, proj_errs, preferred_element_type=jnp.float32).reshape(SEQS, SEQ_LEN, RANK)
    seq_grads = (jnp.einsum("sti,stk->sik", err_proj, act_proj, precision=highest) / SEQ_LEN)
    seq_grads = seq_grads.reshape(SEQS, ENTRIES).astype(jnp.bfloat16)
    gram_sum = lax.dot_general(seq_grads, seq_grads, (((0,), (0,)), ((), ())), preferred_element_type=jnp.float32)
    diag_index = jnp.arange(ENTRIES)
    damped = (fisher + gram_sum / SEQS).at[diag_index, diag_index].add(ridge_damp)
    rhs = queries.reshape(ENTRIES, QUERIES)

    def apply_op(vector):
        return jnp.dot(damped, vector, precision=highest, preferred_element_type=jnp.float32)

    solution, residual = chebyshev(apply_op, rhs)
    scores = jnp.dot(seq_grads.astype(jnp.float32), solution, precision=highest, preferred_element_type=jnp.float32)
    return (solution.reshape(N_SEQ, ENTRIES // N_SEQ, QUERIES), residual.reshape(N_SEQ, ENTRIES // N_SEQ, QUERIES), scores)
```

```python
import jax
import jax.numpy as jnp
from jax import lax
from jax.experimental import pallas as pl
from jax.experimental.pallas import tpu as pltpu
from jax.sharding import PartitionSpec as P

MESH = pl.DeviceIdType.MESH
F32 = jnp.float32
BF16 = jnp.bfloat16

SEQ_LEN = 64
SEQS = 256
NW = 8
NQ = 16
BLK = 128

ridge_damp = 0.1
bound_low = 0.5
bound_high = 6.0
center = 0.5 * (bound_high + bound_low)
half_width = 0.5 * (bound_high - bound_low)
rho_first = half_width / center
rho_second = 1.0 / (2.0 * center / half_width - rho_first)
coef_one = rho_second * rho_first
coef_res = 2.0 * rho_second / half_width

(
    S_V, S_PJ, S_HV, S_VT, S_VF, S_GIVE, S_Y, S_D, S_P, S_PF, S_HY, S_G, S_GF, S_T1, S_T1A, S_GO, S_T2, S_T2A, S_Z,
) = range(19)
(
    R_V, R_PJ, R_HV, R_VT, R_VT1, R_VT2, R_VF, R_GIVE, R_Y, R_D, R_P, R_P1, R_P2, R_PF, R_HY,
    R_G, R_G1, R_G2, R_GF, R_T1, R_T1A, R_GO, R_T2, R_T2A, R_Z,
) = range(25)

NN = (((1,), (0,)), ((), ()))
NT = (((1,), (1,)), ((), ()))
TN = (((0,), (0,)), ((), ()))


def mm(a, b, dims):
    return lax.dot_general(a, b, dims, preferred_element_type=F32)


def kernel(
    act_hbm, err_hbm, pa_hbm, pe_hbm, fish_hbm, q_hbm,
    sol_ref, res_ref, sc_ref,
    actv, errv, pav, pev, fv, fb, qv,
    psend, precv, vsrc, vr, vc, pc, rt,
    ykeep, ygive, ytake, ysend, yrecv, yback, yown, zsend, zrecv,
    gown, dbuf, dwide, panel, gmine,
    t1send, t1part, t1all, t2send, t2part, t2all,
    ld_act, ld_err, ld_w, ld_f, ss, rs,
):
    w = lax.axis_index("width")
    q = lax.axis_index("seq")
    core = lax.rem(q, 2)
    pair = q // 2
    zl = w // 4
    xw = lax.rem(w, 4)
    sib = q + 1 - 2 * core
    diag = w == pair

    def rcopy(src, dst, ssem, rsem, dev):
        return pltpu.make_async_remote_copy(
            src_ref=src, dst_ref=dst, send_sem=ss.at[ssem], recv_sem=rs.at[rsem], device_id=dev, device_id_type=MESH
        )

    def send(src, dst, ssem, rsem, dev):
        rcopy(src, dst, ssem, rsem, dev).start()

    def took(ref, rsem):
        rcopy(ref, ref, 0, rsem, (w, sib)).wait_recv()

    def left(ref, ssem):
        rcopy(ref, ref, ssem, 0, (w, sib)).wait_send()

    def each(lo, hi, body):
        def step(i, carry):
            body(i)
            return carry

        lax.fori_loop(lo, hi, step, 0)

    def ds(start, size, unit):
        return pl.ds(pl.multiple_of(start, unit), size)

    def wpeer(d):
        return lax.rem(w + d, NW)

    def qpeer(d):
        return lax.rem(q + d, NQ)

    def load_block(h):
        return lax.rem(1 - zl + h // 2, 2) * 2 + lax.rem(h, 2)

    def load_rows(h):
        return ds(load_block(h) * 256, 256, 256)

    def act_load(h):
        return pltpu.make_async_copy(act_hbm.at[load_rows(h), :], actv.at[load_rows(h), :], ld_act.at[h])

    def err_load(h):
        return pltpu.make_async_copy(err_hbm.at[load_rows(h), :], errv.at[load_rows(h), :], ld_err.at[h])

    def f_load(j):
        rows = ds(j * 256, 256, 256)
        return pltpu.make_async_copy(fish_hbm.at[rows, :], fv.at[rows, :], ld_f.at[j])

    q_load = pltpu.make_async_copy(q_hbm.at[0], qv, ld_w.at[0])
    pa_load = pltpu.make_async_copy(pa_hbm, pav, ld_w.at[1])
    pe_load = pltpu.make_async_copy(pe_hbm, pev, ld_w.at[2])
    q_load.start()
    pa_load.start()
    pe_load.start()
    for h in range(2):
        act_load(h).start()
        err_load(h).start()

    barrier = pltpu.get_barrier_semaphore()

    def signal(dev):
        pl.semaphore_signal(barrier, inc=1, device_id=dev, device_id_type=MESH)

    each(1, NW, lambda d: signal((lax.rem(w + d, NW), q)))
    each(1, NQ, lambda d: signal((w, lax.rem(q + d, NQ))))
    hold_w, hold_q = q // 2, core * 8 + w
    from_w, from_q = lax.rem(q, 8), 2 * w + q // 8
    keeps = jnp.logical_and(hold_w == w, hold_q == q)
    moves = jnp.logical_not(keeps)

    @pl.when(moves)
    def _():
        signal((hold_w, hold_q))
        signal((from_w, from_q))

    q_load.wait()
    step_one = qv[...] / center
    vsrc[...] = step_one.T.astype(BF16)

    def cols(block):
        return (slice(None), ds(block * BLK, BLK, BLK))

    zq = qpeer(8)

    def y_peer(d):
        return q // 8 * 8 + lax.rem(q + 2 * d, 8)

    def tile(view, some, ssem, rsem):
        def hand(i):
            send(view(i), view(i), ssem + 1, rsem + 3, (w, sib))

        def start():
            send(view(q), view(q), ssem, rsem, (w, zq))
            each(1, 4, lambda d: send(view(q), view(q), ssem, rsem + 1, (w, y_peer(d))))
            hand(q)

        def relay():
            took(some(1), rsem)
            each(1, 4, lambda d: send(view(zq), view(zq), ssem, rsem + 2, (w, y_peer(d))))
            hand(zq)

        def forward():
            took(some(3), rsem + 1)
            each(1, 4, lambda d: hand(y_peer(d)))
            took(some(3), rsem + 2)
            each(1, 4, lambda d: hand(lax.rem(y_peer(d) + 8, NQ)))

        def done():
            took(some(8), rsem + 3)

        def drain():
            left(some(7), ssem)
            left(some(8), ssem + 1)

        return start, relay, forward, done, drain

    def col_some(ref):
        return lambda n: ref.at[:, 0:n * BLK]

    v_start, v_relay, v_forward, v_done, v_drain = tile(lambda i: vc.at[cols(i)], col_some(vc), S_VT, R_VT)
    p_start, p_relay, p_forward, p_done, p_drain = tile(lambda i: pc.at[cols(i)], col_some(pc), S_P, R_P)
    g_start, g_relay, g_forward, g_done, g_drain = tile(
        lambda i: panel.at[ds(i * 16, 16, 16), :], lambda n: panel.at[0:n * 16, :], S_G, R_G
    )

    def project(h):
        rows = load_rows(h)
        psend[rows, 0:128] = mm(actv[rows, :], pav[...], NN)
        psend[rows, 128:256] = mm(errv[rows, :], pev[...], NN)

    def project_send(h):
        def step(d):
            dest = load_block(h) * 2 + lax.rem(xw + d, 2)

            @pl.when(dest != w)
            def _():
                send(psend.at[ds(dest * BLK, BLK, BLK), :], precv.at[w], S_PJ, R_PJ, (dest, q))

        each(0, 2, step)

    def load_wait(h):
        act_load(h).wait()
        err_load(h).wait()

    pa_load.wait()
    pe_load.wait()
    load_wait(0)
    for h in (2, 3):
        act_load(h).start()
        err_load(h).start()
    project(0)

    pl.semaphore_wait(barrier, (NW - 1) + (NQ - 1) + 2 * moves.astype(jnp.int32))

    vr[cols(w)] = vsrc[...]
    each(1, NW, lambda d: send(vsrc, vr.at[cols(w)], S_V, R_V, (wpeer(d), q)))

    @pl.when(moves)
    def _():
        send(vsrc, vc.at[cols(hold_q)], S_HV, R_HV, (hold_w, hold_q))

    @pl.when(keeps)
    def _():
        vc[cols(q)] = vsrc[...]

    project_send(0)
    load_wait(1)
    project(1)
    project_send(1)
    load_wait(2)
    for j in range(4):
        f_load(j).start()
    project(2)
    project_send(2)
    load_wait(3)
    project(3)
    project_send(3)

    def cast_f(j):
        @pl.when(lax.rem(j, 2) == 0)
        def _():
            f_load(j // 2).wait()

        rows = ds(j * BLK, BLK, BLK)
        fb[rows, :] = fv[rows, :].astype(BF16)

        @pl.when(diag)
        def _():
            mid = ds(core * 1024 + j * BLK, BLK, BLK)
            eye = lax.broadcasted_iota(jnp.int32, (BLK, BLK), 0) == lax.broadcasted_iota(jnp.int32, (BLK, BLK), 1)
            fb[rows, mid] = (fv[rows, mid] - jnp.where(eye, center, 0.0)).astype(BF16)

    each(0, 8, cast_f)

    def width_sum(own, recv):
        total = own
        for d in range(1, NW):
            total = total + recv[wpeer(d)].astype(F32)
        return total

    took(vr.at[:, 0:7 * BLK], R_V)

    def apply_transposed(m):
        both = mm(vr[...], fb[:, ds(m * 256, 256, 256)], NN)
        even, odd = both[:, 0:128], both[:, 128:256]
        first = core == 0
        ykeep[m] = jnp.where(first, even, odd)
        ygive[m] = jnp.where(first, odd, even).astype(BF16)

    each(0, 8, apply_transposed)
    send(ygive, ytake, S_GIVE, R_GIVE, (w, sib))
    @pl.when(moves)
    def _():
        took(vc.at[cols(q)], R_HV)

    v_start()
    took(ytake, R_GIVE)

    def y_send(d):
        m = lax.rem(pair + d, 8)
        ysend[m] = (ykeep[m] + ytake[m].astype(F32)).astype(BF16)
        send(ysend.at[m], yrecv.at[pair], S_Y, R_Y, (w, 2 * m + core))

    each(1, 8, y_send)

    own_rows = ds(w * BLK, BLK, BLK)
    took(precv.at[0:7], R_PJ)
    projected = width_sum(psend[own_rows, :], precv)
    for s in range(2):
        act = projected[s * SEQ_LEN:(s + 1) * SEQ_LEN, 0:128]
        err = projected[s * SEQ_LEN:(s + 1) * SEQ_LEN, 128:256]
        grad = lax.dot_general(
            err.T, act, NN, precision=lax.Precision.HIGHEST, preferred_element_type=F32
        )
        gown[s] = (grad / SEQ_LEN).astype(BF16)

    def grad_send(d):
        i = wpeer(d)
        send(gown.at[:, ds(i * 16, 16, 16), :], dbuf.at[pl.ds(2 * w, 2)], S_D, R_D, (i, q))

    each(1, NW, grad_send)
    dbuf[pl.ds(2 * w, 2)] = gown[:, ds(w * 16, 16, 16), :]

    v_relay()
    took(yrecv.at[0:7], R_Y)
    y_block = ykeep[pair] + ytake[pair].astype(F32)
    for d in range(1, 8):
        y_block = y_block + yrecv[lax.rem(pair + d, 8)].astype(F32)
    yback[...] = y_block
    pc[cols(q)] = (-y_block - ridge_damp * vc[cols(q)].astype(F32)).astype(BF16)
    p_start()

    @pl.when(moves)
    def _():
        send(yback, yown, S_HY, R_HY, (from_w, from_q))

    @pl.when(keeps)
    def _():
        yown[...] = y_block

    took(dbuf.at[0:14], R_D)
    dwide[...] = dbuf[...].astype(F32)
    seq_rows = ds(q * 16, 16, 16)
    for i in range(16):
        panel[seq_rows, i * BLK:(i + 1) * BLK] = dwide[:, i, :].astype(BF16)

    g_start()

    def seq_products(vt, out, part, ssem, rsem):
        value = mm(panel[seq_rows, :], vt[...], NT)
        out[...] = value
        part[w] = value
        each(1, NW, lambda d: send(out, part.at[w], ssem, rsem, (wpeer(d), q)))

    def seq_gather(part, whole, rsem, asem, arsem):
        took(part.at[0:7], rsem)
        total = part[0]
        for i in range(1, NW):
            total = total + part[i]
        whole[seq_rows, :] = total
        mine = whole.at[seq_rows, :]
        each(1, NQ, lambda d: send(mine, mine, asem, arsem, (w, qpeer(d))))

    v_forward()
    v_done()
    seq_products(vc, t1send, t1part, S_T1, R_T1)
    p_relay()
    g_relay()
    seq_gather(t1part, t1all, R_T1, S_T1A, R_T1A)
    p_forward()
    g_forward()
    p_done()
    took(t1all.at[0:240, :], R_T1A)
    g_done()

    @pl.when(moves)
    def _():
        send(panel.at[:, ds(q * BLK, BLK, BLK)], gmine, S_GO, R_GO, (from_w, from_q))

    @pl.when(keeps)
    def _():
        gmine[...] = panel[:, ds(q * BLK, BLK, BLK)]

    t1b = t1all[...].astype(BF16)
    for k in range(4):
        part = slice(k * 512, (k + 1) * 512)
        wt = mm(t1b, panel[:, part], TN)
        rt[:, part] = (pc[:, part].astype(F32) - wt / SEQS).astype(BF16)
    seq_products(rt, t2send, t2part, S_T2, R_T2)

    def apply_rows(j):
        rows = ds(j * 512, 512, 512)
        zsend[rows, :] = mm(fb[rows, :], rt[...], NT).astype(BF16)

    each(0, 2, apply_rows)
    each(1, NW, lambda d: send(zsend.at[ds(wpeer(d) * BLK, BLK, BLK), :], zrecv.at[w], S_Z, R_Z, (wpeer(d), q)))
    seq_gather(t2part, t2all, R_T2, S_T2A, R_T2A)

    @pl.when(moves)
    def _():
        took(gmine, R_GO)
        took(yown, R_HY)

    one = qv[...] / center
    y_shift = yown[...].T
    w_own = mm(gmine[...], t1b, TN) / SEQS
    res_one = -y_shift - ridge_damp * one - w_own
    step_two = coef_one * one + coef_res * res_one
    sol_ref[0] = one + step_two

    left(vr.at[:, 0:7 * BLK], S_V)
    left(precv.at[0:7], S_PJ)
    v_drain()
    left(ygive, S_GIVE)
    left(ysend.at[0:7], S_Y)
    left(dbuf.at[0:14], S_D)
    p_drain()
    g_drain()
    left(t1part.at[0:7], S_T1)
    left(t1all.at[0:240, :], S_T1A)
    left(t2part.at[0:7], S_T2)

    @pl.when(moves)
    def _():
        left(vsrc, S_HV)
        left(yback, S_HY)
        left(gmine, S_GO)

    took(zrecv.at[0:7], R_Z)
    z_own = center * res_one + width_sum(zsend[own_rows, :].astype(F32), zrecv)
    f_two = coef_one * (center * one + y_shift) + coef_res * z_own
    base = res_one - f_two - ridge_damp * step_two - coef_one * w_own

    took(t2all.at[0:240, :], R_T2A)
    g_two = mm(gmine[...], t2all[...].astype(BF16), TN) / SEQS
    res_ref[0] = base - coef_res * g_two
    score_rows = pl.ds(2 * (w * NQ + q), 2)
    sc_ref[...] = (1.0 + coef_one) * t1all[score_rows, :] + coef_res * t2all[score_rows, :]
    left(zrecv.at[0:7], S_Z)
    left(t2all.at[0:240, :], S_T2A)


def settle(sol_in, res_in, sc_in, sol_ref, res_ref, sc_ref):
    sol_ref[...] = sol_in[...]
    res_ref[...] = res_in[...]
    sc_ref[...] = sc_in[...]


def on_device(activations, errors, proj_acts, proj_errs, fisher, queries):
    vm = pltpu.VMEM
    dma = pltpu.SemaphoreType.DMA
    scratch = [
        vm((1024, 3584), BF16), vm((1024, 1024), BF16), vm((3584, 128), BF16), vm((1024, 128), BF16),
        vm((1024, 2048), F32), vm((1024, 2048), BF16), vm((128, 128), F32),
        vm((1024, 256), F32), vm((8, 128, 256), F32),
        vm((128, 128), BF16), vm((128, 1024), BF16), vm((128, 2048), BF16), vm((128, 2048), BF16), vm((128, 2048), BF16),
        vm((8, 128, 128), F32), vm((8, 128, 128), BF16), vm((8, 128, 128), BF16), vm((8, 128, 128), BF16),
        vm((8, 128, 128), BF16), vm((128, 128), F32), vm((128, 128), F32), vm((1024, 128), BF16), vm((8, 128, 128), BF16),
        vm((2, 128, 128), BF16), vm((16, 16, 128), BF16), vm((16, 16, 128), F32), vm((256, 2048), BF16), vm((256, 128), BF16),
        vm((16, 128), F32), vm((8, 16, 128), F32), vm((256, 128), F32),
        vm((16, 128), F32), vm((8, 16, 128), F32), vm((256, 128), F32),
        dma((4,)), dma((4,)), dma((3,)), dma((4,)), dma((19,)), dma((25,)),
    ]
    hbm = pl.BlockSpec(memory_space=pl.ANY)
    vmem = pl.BlockSpec(memory_space=pltpu.VMEM)
    raw = pl.pallas_call(
        kernel,
        out_shape=(
            jax.ShapeDtypeStruct((1, 128, 128), F32),
            jax.ShapeDtypeStruct((1, 128, 128), F32),
            jax.ShapeDtypeStruct((2, 128), F32),
        ),
        in_specs=[hbm] * 6,
        out_specs=(vmem, vmem, vmem),
        scratch_shapes=scratch,
        compiler_params=pltpu.CompilerParams(
            collective_id=0, has_side_effects=True, vmem_limit_bytes=56 * 1024 * 1024
        ),
    )(activations, errors, proj_acts, proj_errs, fisher, queries)
    return pl.pallas_call(
        settle,
        out_shape=tuple(jax.ShapeDtypeStruct(r.shape, r.dtype) for r in raw),
        in_specs=[vmem] * 3,
        out_specs=(vmem, vmem, vmem),
    )(*raw)


def solution(mesh):
    placed = (
        P("seq", "width"),
        P("seq", "width"),
        P("width", None),
        P("width", None),
        P("seq", "width"),
        P("seq", "width", None),
    )
    return jax.shard_map(
        on_device,
        mesh=mesh,
        in_specs=placed,
        out_specs=(P("seq", "width", None), P("seq", "width", None), P(("width", "seq"), None)),
        check_vma=False,
    )
```

```python
import jax
import jax.numpy as jnp
from jax import lax
from jax.experimental import pallas as pl
from jax.experimental.pallas import tpu as pltpu
from jax.sharding import PartitionSpec as P

MESH = pl.DeviceIdType.MESH
F32 = jnp.float32
BF16 = jnp.bfloat16

SEQ_LEN = 64
SEQS = 256
NW = 8
NQ = 16
BLK = 128

ridge_damp = 0.1
bound_low = 0.5
bound_high = 6.0
center = 0.5 * (bound_high + bound_low)
half_width = 0.5 * (bound_high - bound_low)
rho_first = half_width / center
rho_second = 1.0 / (2.0 * center / half_width - rho_first)
coef_one = rho_second * rho_first
coef_res = 2.0 * rho_second / half_width

(
    S_V, S_PJ, S_HV, S_VT, S_VF, S_GIVE, S_Y, S_D, S_P, S_PF, S_HY, S_G, S_GF, S_T1, S_T1A, S_GO, S_T2, S_T2A, S_Z, S_PE, S_PA2, S_PE2, S_SC, S_PB, S_PBF, S_GB, S_GBF,
) = range(27)
(
    R_V, R_PJ, R_HV, R_VT, R_VT1, R_VT2, R_VF, R_GIVE, R_Y, R_D, R_P, R_P1, R_P2, R_PF, R_HY,
    R_G, R_G1, R_G2, R_GF, R_T1, R_T1A, R_GO, R_T2, R_T2A, R_Z, R_PE, R_PA2, R_PE2, R_SC,
    R_PB, R_PB1, R_PB2, R_PBF, R_GB, R_GB1, R_GB2, R_GBF, R_PJB, R_PEB,
) = range(39)

NN = (((1,), (0,)), ((), ()))
NT = (((1,), (1,)), ((), ()))
TN = (((0,), (0,)), ((), ()))


def mm(a, b, dims):
    return lax.dot_general(a, b, dims, preferred_element_type=F32)


def kernel(
    act_hbm, err_hbm, pa_hbm, pe_hbm, fish_hbm, q_hbm,
    sol_ref, res_ref, sc_ref,
    actv, errv, pav, pev, fv, fb, qv,
    pa, pe, ra, re, sa, se, ra2, re2, vsrc, vr, vc, pc, rt,
    ykeep, ygive, ytake, ysend, yrecv, yback, yown, zsend, zrecv,
    gown, dbuf, dwide, panel, gmine,
    t1send, t1part, t1sum, t1all, t2send, t2part, t2all, score, smine,
    ld_act, ld_err, ld_w, ld_f, ss, rs,
):
    w = lax.axis_index("width")
    q = lax.axis_index("seq")
    core = lax.rem(q, 2)
    pair = q // 2
    zl = w // 4
    xw = lax.rem(w, 4)
    sib = q + 1 - 2 * core
    diag = w == pair

    def rcopy(src, dst, ssem, rsem, dev):
        return pltpu.make_async_remote_copy(
            src_ref=src, dst_ref=dst, send_sem=ss.at[ssem], recv_sem=rs.at[rsem], device_id=dev, device_id_type=MESH
        )

    def send(src, dst, ssem, rsem, dev):
        rcopy(src, dst, ssem, rsem, dev).start()

    def took(ref, rsem):
        rcopy(ref, ref, 0, rsem, (w, sib)).wait_recv()

    def left(ref, ssem):
        rcopy(ref, ref, ssem, 0, (w, sib)).wait_send()

    def each(lo, hi, body):
        def step(i, carry):
            body(i)
            return carry

        lax.fori_loop(lo, hi, step, 0)

    def ds(start, size, unit):
        return pl.ds(pl.multiple_of(start, unit), size)

    def wpeer(d):
        return lax.rem(w + d, NW)

    def qpeer(d):
        return lax.rem(q + d, NQ)

    far_w = [
        lax.rem(zl + dz, 2) * 4 + lax.rem(xw + dx, 4)
        for dz, dx in ((1, 2), (1, 1), (1, 3), (0, 2), (1, 0), (0, 1), (0, 3))
    ]
    far_q = [
        lax.rem(q // 8 + dz, 2) * 8 + lax.rem(q // 2 + dy, 4) * 2 + lax.rem(core + dc, 2)
        for dz, dy in ((1, 2), (1, 1), (1, 3), (1, 0), (0, 2), (0, 1), (0, 3), (0, 0))
        for dc in ((0, 1) if dz + dy else (1,))
    ]

    def load_block(h):
        return lax.rem(1 - zl + h // 2, 2) * 2 + lax.rem(h, 2)

    def load_rows(h):
        return ds(load_block(h) * 256, 256, 256)

    def act_load(h):
        return pltpu.make_async_copy(act_hbm.at[load_rows(h), :], actv.at[load_rows(h), :], ld_act.at[h])

    def err_load(h):
        return pltpu.make_async_copy(err_hbm.at[load_rows(h), :], errv.at[load_rows(h), :], ld_err.at[h])

    def f_load(j):
        rows = ds(j * 256, 256, 256)
        return pltpu.make_async_copy(fish_hbm.at[rows, :], fv.at[rows, :], ld_f.at[j])

    q_load = pltpu.make_async_copy(q_hbm.at[0], qv, ld_w.at[0])
    pa_load = pltpu.make_async_copy(pa_hbm, pav, ld_w.at[1])
    pe_load = pltpu.make_async_copy(pe_hbm, pev, ld_w.at[2])
    q_load.start()
    pa_load.start()
    pe_load.start()
    for h in range(2):
        act_load(h).start()
        err_load(h).start()

    barrier = pltpu.get_barrier_semaphore()

    def signal(dev):
        pl.semaphore_signal(barrier, inc=1, device_id=dev, device_id_type=MESH)

    each(1, NW, lambda d: signal((lax.rem(w + d, NW), q)))
    each(1, NQ, lambda d: signal((w, lax.rem(q + d, NQ))))
    hold_w, hold_q = q // 2, core * 8 + w
    from_w, from_q = lax.rem(q, 8), 2 * w + q // 8
    keeps = jnp.logical_and(hold_w == w, hold_q == q)
    moves = jnp.logical_not(keeps)

    @pl.when(moves)
    def _():
        signal((hold_w, hold_q))
        signal((from_w, from_q))

    q_load.wait()
    step_one = qv[...] / center
    vsrc[...] = step_one.T.astype(BF16)

    def cols(block):
        return (slice(None), ds(block * BLK, BLK, BLK))

    zq = qpeer(8)

    def y_peer(d):
        return q // 8 * 8 + lax.rem(q + 2 * d, 8)

    def over(i):
        return lax.rem(i + 8, NQ)

    def tile(view, some, ssem, rsem, y_first=False):
        def hand(i):
            send(view(i), view(i), ssem + 1, rsem + 3, (w, sib))

        def along_y():
            each(1, 4, lambda d: send(view(q), view(q), ssem, rsem + 1, (w, y_peer(d))))

        def along_z():
            send(view(q), view(q), ssem, rsem, (w, zq))

        def start():
            (along_y if y_first else along_z)()

        def rest():
            (along_z if y_first else along_y)()
            hand(q)

        def relay():
            if y_first:
                took(some(3), rsem + 1)

                def step(d):
                    i = y_peer(d)
                    send(view(i), view(i), ssem, rsem + 2, (w, zq))
                    hand(i)

                each(1, 4, step)
            else:
                took(some(1), rsem)
                each(1, 4, lambda d: send(view(zq), view(zq), ssem, rsem + 2, (w, y_peer(d))))
                hand(zq)

        def forward():
            if y_first:
                took(some(1), rsem)
                hand(zq)
            else:
                took(some(3), rsem + 1)
                each(1, 4, lambda d: hand(y_peer(d)))
            took(some(3), rsem + 2)
            each(1, 4, lambda d: hand(over(y_peer(d))))

        def done():
            took(some(8), rsem + 3)

        def drain():
            left(some(7), ssem)
            left(some(8), ssem + 1)

        return start, rest, relay, forward, done, drain

    def halves(first, second):
        def both(pair_of):
            def run():
                for f in pair_of:
                    f()

            return run

        return [both(pair_of) for pair_of in zip(first, second)]

    def pc_half(r):
        return (lambda i: pc.at[r * 64:(r + 1) * 64, ds(i * BLK, BLK, BLK)], lambda n: pc.at[0:64, 0:n * BLK])

    def panel_half(r):
        return (
            lambda i: panel.at[ds(i * 16, 16, 16), r * 1024:(r + 1) * 1024],
            lambda n: panel.at[0:n * 16, 0:1024],
        )

    v_start, v_rest, v_relay, v_forward, v_done, v_drain = tile(lambda i: vc.at[cols(i)], lambda n: vc.at[:, 0:n * BLK], S_VT, R_VT)
    p_start, p_rest, p_relay, p_forward, p_done, p_drain = halves(
        tile(*pc_half(0), S_P, R_P), tile(*pc_half(1), S_PB, R_PB, True)
    )
    g_start, g_rest, g_relay, g_forward, g_done, g_drain = halves(
        tile(*panel_half(0), S_G, R_G), tile(*panel_half(1), S_GB, R_GB, True)
    )

    zw = wpeer(4)

    def x_peer(d):
        return zl * 4 + lax.rem(xw + d, 4)

    def project(h):
        rows = load_rows(h)
        pa[rows, :] = mm(actv[rows, :], pav[...], NN)
        pe[rows, :] = mm(errv[rows, :], pev[...], NN)

    def token_rows(block):
        return ds(block * BLK, BLK, BLK)

    def project_send(h):
        if h < 2:
            send(pa.at[load_rows(h), :], ra.at[h * 256:(h + 1) * 256, :], S_PJ, (R_PJ, R_PJB)[h], (zw, q))
        half = lax.rem(1 - zl + h // 2, 2)

        def step(d):
            x = h % 2 * 2 + lax.rem(xw + d, 2)

            @pl.when(x != xw)
            def _():
                send(pe.at[token_rows(half * 4 + x), :], re.at[xw, half], S_PE, (R_PE, R_PEB)[h // 2], (zl * 4 + x, q))

        each(0, 2, step)

    def project_act(h):
        took(ra.at[0:256, :], (R_PJ, R_PJB)[h])

        def step(d):
            x = h * 2 + lax.rem(xw + d, 2)
            sa[x] = pa[token_rows(zl * 4 + x), :] + ra[token_rows(x), :]

            @pl.when(x != xw)
            def _():
                send(sa.at[x], ra2.at[xw], S_PA2, R_PA2, (zl * 4 + x, q))

        each(0, 2, step)

    def err_half(half):
        total = pe[token_rows(half * 4 + xw), :]
        for d in range(1, 4):
            total = total + re[lax.rem(xw + d, 4), half]
        return total

    def project_err():
        took(re.at[0:3, 0], R_PE)
        se[...] = err_half(1 - zl)
        send(se, re2, S_PE2, R_PE2, (zw, q))

    def project_total():
        took(re.at[0:3, 0], R_PEB)
        err = err_half(zl)
        took(re2, R_PE2)
        err = err + re2[...]
        took(ra2.at[0:3], R_PA2)
        act = sa[xw]
        for d in range(1, 4):
            act = act + ra2[lax.rem(xw + d, 4)]
        return act, err

    def load_wait(h):
        act_load(h).wait()
        err_load(h).wait()

    pa_load.wait()
    pe_load.wait()
    load_wait(0)
    for h in (2, 3):
        act_load(h).start()
        err_load(h).start()
    project(0)

    pl.semaphore_wait(barrier, (NW - 1) + (NQ - 1) + 2 * moves.astype(jnp.int32))

    vr[cols(w)] = vsrc[...]
    each(1, NW, lambda d: send(vsrc, vr.at[cols(w)], S_V, R_V, (wpeer(d), q)))

    @pl.when(moves)
    def _():
        send(vsrc, vc.at[cols(hold_q)], S_HV, R_HV, (hold_w, hold_q))

    @pl.when(keeps)
    def _():
        vc[cols(q)] = vsrc[...]

    project_send(0)
    load_wait(1)
    project(1)
    project_send(1)
    load_wait(2)
    for j in range(4):
        f_load(j).start()
    project(2)
    project_send(2)
    load_wait(3)
    project(3)
    project_send(3)

    def cast_f(j):
        @pl.when(lax.rem(j, 2) == 0)
        def _():
            f_load(j // 2).wait()

        rows = ds(j * BLK, BLK, BLK)
        fb[rows, :] = fv[rows, :].astype(BF16)

        @pl.when(diag)
        def _():
            mid = ds(core * 1024 + j * BLK, BLK, BLK)
            eye = lax.broadcasted_iota(jnp.int32, (BLK, BLK), 0) == lax.broadcasted_iota(jnp.int32, (BLK, BLK), 1)
            fb[rows, mid] = (fv[rows, mid] - jnp.where(eye, center, 0.0)).astype(BF16)

    each(0, 8, cast_f)

    def width_sum(own, recv):
        total = own
        for d in range(1, NW):
            total = total + recv[wpeer(d)].astype(F32)
        return total

    took(vr.at[:, 0:7 * BLK], R_V)

    def apply_transposed(m):
        both = mm(vr[...], fb[:, ds(m * 256, 256, 256)], NN)
        even, odd = both[:, 0:128], both[:, 128:256]
        first = core == 0
        ykeep[m] = jnp.where(first, even, odd)
        ygive[m] = jnp.where(first, odd, even).astype(BF16)

    each(0, 8, apply_transposed)
    send(ygive, ytake, S_GIVE, R_GIVE, (w, sib))
    @pl.when(moves)
    def _():
        took(vc.at[cols(q)], R_HV)

    v_start()
    v_rest()
    project_act(0)
    project_err()
    project_act(1)
    took(ytake, R_GIVE)

    def y_send(d):
        m = lax.rem(pair + d, 8)
        ysend[m] = (ykeep[m] + ytake[m].astype(F32)).astype(BF16)
        send(ysend.at[m], yrecv.at[pair], S_Y, R_Y, (w, 2 * m + core))

    each(1, 8, y_send)

    v_relay()
    own_rows = ds(w * BLK, BLK, BLK)
    act_sum, err_sum = project_total()
    for s in range(2):
        act = act_sum[s * SEQ_LEN:(s + 1) * SEQ_LEN, :]
        err = err_sum[s * SEQ_LEN:(s + 1) * SEQ_LEN, :]
        grad = lax.dot_general(
            err.T, act, NN, precision=lax.Precision.HIGHEST, preferred_element_type=F32
        )
        gown[s] = (grad / SEQ_LEN).astype(BF16)

    for i in far_w:
        send(gown.at[:, ds(i * 16, 16, 16), :], dbuf.at[pl.ds(2 * w, 2)], S_D, R_D, (i, q))

    dbuf[pl.ds(2 * w, 2)] = gown[:, ds(w * 16, 16, 16), :]

    took(yrecv.at[0:7], R_Y)
    y_block = ykeep[pair] + ytake[pair].astype(F32)
    for d in range(1, 8):
        y_block = y_block + yrecv[lax.rem(pair + d, 8)].astype(F32)
    yback[...] = y_block
    pc[cols(q)] = (-y_block - ridge_damp * vc[cols(q)].astype(F32)).astype(BF16)
    p_start()
    p_rest()

    @pl.when(moves)
    def _():
        send(yback, yown, S_HY, R_HY, (from_w, from_q))

    @pl.when(keeps)
    def _():
        yown[...] = y_block

    v_forward()
    took(dbuf.at[0:14], R_D)
    dwide[...] = dbuf[...].astype(F32)
    seq_rows = ds(q * 16, 16, 16)
    for i in range(16):
        panel[seq_rows, i * BLK:(i + 1) * BLK] = dwide[:, i, :].astype(BF16)

    g_start()
    g_rest()

    def seq_products(value, out, part, ssem, rsem):
        out[...] = value
        part[w] = value
        for i in far_w:
            send(out, part.at[w], ssem, rsem, (i, q))

    def seq_gather(part, whole, rsem, asem, arsem):
        took(part.at[0:7], rsem)
        total = part[0]
        for i in range(1, NW):
            total = total + part[i]
        whole[seq_rows, :] = total.astype(BF16)
        mine = whole.at[seq_rows, :]
        for i in far_q:
            send(mine, mine, asem, arsem, (w, i))
        return total

    v_done()
    seq_products(mm(panel[seq_rows, :], vc[...], NT), t1send, t1part, S_T1, R_T1)
    p_relay()
    g_relay()
    t1sum[...] = seq_gather(t1part, t1all, R_T1, S_T1A, R_T1A)
    p_forward()
    g_forward()
    p_done()
    g_done()

    @pl.when(moves)
    def _():
        send(panel.at[:, ds(q * BLK, BLK, BLK)], gmine, S_GO, R_GO, (from_w, from_q))

    @pl.when(keeps)
    def _():
        gmine[...] = panel[:, ds(q * BLK, BLK, BLK)]

    kpart = mm(panel[seq_rows, :], panel[...], NT).astype(BF16)
    gpart = mm(panel[seq_rows, :], pc[...], NT)
    took(t1all.at[0:240, :], R_T1A)
    t1b = t1all[...]
    seq_products(gpart - mm(kpart, t1b, NN) / SEQS, t2send, t2part, S_T2, R_T2)
    for k in range(4):
        part = slice(k * 512, (k + 1) * 512)
        wt = mm(t1b, panel[:, part], TN)
        rt[:, part] = (pc[:, part].astype(F32) - wt / SEQS).astype(BF16)

    def apply_rows(j):
        rows = ds(j * 512, 512, 512)
        zsend[rows, :] = mm(fb[rows, :], rt[...], NT).astype(BF16)

    each(0, 2, apply_rows)
    each(1, NW, lambda d: send(zsend.at[ds(wpeer(d) * BLK, BLK, BLK), :], zrecv.at[w], S_Z, R_Z, (wpeer(d), q)))
    t2sum = seq_gather(t2part, t2all, R_T2, S_T2A, R_T2A)
    score[...] = (1.0 + coef_one) * t1sum[...] + coef_res * t2sum

    @pl.when(moves)
    def _():
        send(score, smine, S_SC, R_SC, (hold_w, hold_q))

    @pl.when(keeps)
    def _():
        smine[...] = score[...]

    @pl.when(moves)
    def _():
        took(gmine, R_GO)
        took(yown, R_HY)

    one = qv[...] / center
    y_shift = yown[...].T
    w_own = mm(gmine[...], t1b, TN) / SEQS
    res_one = -y_shift - ridge_damp * one - w_own
    step_two = coef_one * one + coef_res * res_one
    sol_ref[0] = one + step_two

    left(vr.at[:, 0:7 * BLK], S_V)
    left(ra, S_PJ)
    left(re.at[0:3], S_PE)
    left(ra2.at[0:3], S_PA2)
    left(re2, S_PE2)
    v_drain()
    left(ygive, S_GIVE)
    left(ysend.at[0:7], S_Y)
    left(dbuf.at[0:14], S_D)
    p_drain()
    g_drain()
    left(t1part.at[0:7], S_T1)
    left(t1all.at[0:240, :], S_T1A)
    left(t2part.at[0:7], S_T2)

    @pl.when(moves)
    def _():
        left(vsrc, S_HV)
        left(yback, S_HY)
        left(gmine, S_GO)

    took(zrecv.at[0:7], R_Z)
    z_own = center * res_one + width_sum(zsend[own_rows, :].astype(F32), zrecv)
    f_two = coef_one * (center * one + y_shift) + coef_res * z_own
    base = res_one - f_two - ridge_damp * step_two - coef_one * w_own

    took(t2all.at[0:240, :], R_T2A)
    g_two = mm(gmine[...], t2all[...], TN) / SEQS
    res_ref[0] = base - coef_res * g_two

    @pl.when(moves)
    def _():
        took(score, R_SC)
        left(score, S_SC)

    sc_ref[...] = smine[pl.ds(2 * from_w, 2), :]
    left(zrecv.at[0:7], S_Z)
    left(t2all.at[0:240, :], S_T2A)


def settle(sol_in, res_in, sc_in, sol_ref, res_ref, sc_ref, sems):
    copies = [
        pltpu.make_async_copy(src, dst, sems.at[i])
        for i, (src, dst) in enumerate(((sol_in, sol_ref), (res_in, res_ref), (sc_in, sc_ref)))
    ]
    for copy in copies:
        copy.start()
    for copy in copies:
        copy.wait()


def on_device(activations, errors, proj_acts, proj_errs, fisher, queries):
    vm = pltpu.VMEM
    dma = pltpu.SemaphoreType.DMA
    scratch = [
        vm((1024, 3584), BF16), vm((1024, 1024), BF16), vm((3584, 128), BF16), vm((1024, 128), BF16),
        vm((1024, 2048), F32), vm((1024, 2048), BF16), vm((128, 128), F32),
        vm((1024, 128), F32), vm((1024, 128), F32), vm((512, 128), F32), vm((4, 2, 128, 128), F32),
        vm((4, 128, 128), F32), vm((128, 128), F32), vm((4, 128, 128), F32), vm((128, 128), F32),
        vm((128, 128), BF16), vm((128, 1024), BF16), vm((128, 2048), BF16), vm((128, 2048), BF16), vm((128, 2048), BF16),
        vm((8, 128, 128), F32), vm((8, 128, 128), BF16), vm((8, 128, 128), BF16), vm((8, 128, 128), BF16),
        vm((8, 128, 128), BF16), vm((128, 128), F32), vm((128, 128), F32), vm((1024, 128), BF16), vm((8, 128, 128), BF16),
        vm((2, 128, 128), BF16), vm((16, 16, 128), BF16), vm((16, 16, 128), F32), vm((256, 2048), BF16), vm((256, 128), BF16),
        vm((16, 128), F32), vm((8, 16, 128), F32), vm((16, 128), F32), vm((256, 128), BF16),
        vm((16, 128), F32), vm((8, 16, 128), F32), vm((256, 128), BF16), vm((16, 128), F32), vm((16, 128), F32),
        dma((4,)), dma((4,)), dma((3,)), dma((4,)), dma((27,)), dma((39,)),
    ]
    hbm = pl.BlockSpec(memory_space=pl.ANY)
    operands = (activations, errors, proj_acts, proj_errs, fisher, queries)
    vmem = pl.BlockSpec(memory_space=pltpu.VMEM)
    raw = pl.pallas_call(
        kernel,
        out_shape=(
            jax.ShapeDtypeStruct((1, 128, 128), F32),
            jax.ShapeDtypeStruct((1, 128, 128), F32),
            jax.ShapeDtypeStruct((2, 128), F32),
        ),
        in_specs=[hbm] * 6,
        out_specs=(vmem, vmem, vmem),
        scratch_shapes=scratch,
        compiler_params=pltpu.CompilerParams(
            collective_id=0, has_side_effects=True, vmem_limit_bytes=34 * 1024 * 1024
        ),
    )(*[pltpu.with_memory_space_constraint(a, pltpu.HBM) for a in operands])
    return pl.pallas_call(
        settle,
        out_shape=tuple(jax.ShapeDtypeStruct(r.shape, r.dtype) for r in raw),
        in_specs=[hbm] * 3,
        out_specs=(hbm, hbm, hbm),
        scratch_shapes=[dma((3,))],
        compiler_params=pltpu.CompilerParams(vmem_limit_bytes=4 * 1024 * 1024),
    )(*raw)


def solution(mesh):
    placed = (
        P("seq", "width"),
        P("seq", "width"),
        P("width", None),
        P("width", None),
        P("seq", "width"),
        P("seq", "width", None),
    )
    return jax.shard_map(
        on_device,
        mesh=mesh,
        in_specs=placed,
        out_specs=(P("seq", "width", None), P("seq", "width", None), P(("width", "seq"), None)),
        check_vma=False,
    )
```

```python
import jax
import jax.numpy as jnp
from jax import lax
from jax.experimental import pallas as pl
from jax.experimental.pallas import tpu as pltpu
from jax.sharding import PartitionSpec as P

MESH = pl.DeviceIdType.MESH
F32 = jnp.float32
BF16 = jnp.bfloat16

SEQ_LEN = 64
SEQS = 256
NW = 8
NQ = 16
BLK = 128

ridge_damp = 0.1
bound_low = 0.5
bound_high = 6.0
center = 0.5 * (bound_high + bound_low)
half_width = 0.5 * (bound_high - bound_low)
rho_first = half_width / center
rho_second = 1.0 / (2.0 * center / half_width - rho_first)
coef_one = rho_second * rho_first
coef_res = 2.0 * rho_second / half_width

(
    S_V, S_PJ, S_HV, S_VT, S_VF, S_GIVE, S_Y, S_D, S_P, S_PF, S_HY, S_G, S_GF, S_T1, S_T1A, S_GO, S_T2, S_T2A, S_Z, S_PE, S_PA2, S_PE2, S_SC, S_PB, S_PBF, S_GB, S_GBF,
) = range(27)
(
    R_V, R_PJ, R_HV, R_VT, R_VT1, R_VT2, R_VF, R_GIVE, R_Y, R_D, R_P, R_P1, R_P2, R_PF, R_HY,
    R_G, R_G1, R_G2, R_GF, R_T1, R_T1A, R_GO, R_T2, R_T2A, R_Z, R_PE, R_PA2, R_PE2, R_SC,
    R_PB, R_PB1, R_PB2, R_PBF, R_GB, R_GB1, R_GB2, R_GBF, R_PJB, R_PEB,
) = range(39)

NN = (((1,), (0,)), ((), ()))
NT = (((1,), (1,)), ((), ()))
TN = (((0,), (0,)), ((), ()))


def mm(a, b, dims):
    return lax.dot_general(a, b, dims, preferred_element_type=F32)


def kernel(
    act_hbm, err_hbm, pa_hbm, pe_hbm, fish_hbm, q_hbm,
    sol_ref, res_ref, sc_ref,
    actv, errv, pav, pev, fv, fb, qv,
    pa, pe, ra, re, sa, se, ra2, re2, vsrc, vr, vc, pc, rt,
    ykeep, ygive, ytake, ysend, yrecv, yback, yown, zsend, zrecv,
    gown, dbuf, dwide, panel, gmine,
    t1send, t1part, t1sum, t1all, t2send, t2part, t2all, score, smine,
    ld_act, ld_err, ld_w, ld_f, ss, rs,
):
    w = lax.axis_index("width")
    q = lax.axis_index("seq")
    core = lax.rem(q, 2)
    pair = q // 2
    zl = w // 4
    xw = lax.rem(w, 4)
    sib = q + 1 - 2 * core
    diag = w == pair

    def rcopy(src, dst, ssem, rsem, dev):
        return pltpu.make_async_remote_copy(
            src_ref=src, dst_ref=dst, send_sem=ss.at[ssem], recv_sem=rs.at[rsem], device_id=dev, device_id_type=MESH
        )

    def send(src, dst, ssem, rsem, dev):
        rcopy(src, dst, ssem, rsem, dev).start()

    def took(ref, rsem):
        rcopy(ref, ref, 0, rsem, (w, sib)).wait_recv()

    def left(ref, ssem):
        rcopy(ref, ref, ssem, 0, (w, sib)).wait_send()

    def each(lo, hi, body):
        def step(i, carry):
            body(i)
            return carry

        lax.fori_loop(lo, hi, step, 0)

    def ds(start, size, unit):
        return pl.ds(pl.multiple_of(start, unit), size)

    def wpeer(d):
        return lax.rem(w + d, NW)

    def qpeer(d):
        return lax.rem(q + d, NQ)

    far_w = [
        lax.rem(zl + dz, 2) * 4 + lax.rem(xw + dx, 4)
        for dz, dx in ((1, 2), (1, 1), (1, 3), (0, 2), (1, 0), (0, 1), (0, 3))
    ]
    far_q = [
        lax.rem(q // 8 + dz, 2) * 8 + lax.rem(q // 2 + dy, 4) * 2 + lax.rem(core + dc, 2)
        for dz, dy in ((1, 2), (1, 1), (1, 3), (1, 0), (0, 2), (0, 1), (0, 3), (0, 0))
        for dc in ((0, 1) if dz + dy else (1,))
    ]

    def load_block(h):
        return lax.rem(1 - zl + h // 2, 2) * 2 + lax.rem(h, 2)

    def load_rows(h):
        return ds(load_block(h) * 256, 256, 256)

    def act_load(h):
        return pltpu.make_async_copy(act_hbm.at[load_rows(h), :], actv.at[load_rows(h), :], ld_act.at[h])

    def err_load(h):
        return pltpu.make_async_copy(err_hbm.at[load_rows(h), :], errv.at[load_rows(h), :], ld_err.at[h])

    def f_load(j):
        rows = ds(j * 256, 256, 256)
        return pltpu.make_async_copy(fish_hbm.at[rows, :], fv.at[rows, :], ld_f.at[j])

    q_load = pltpu.make_async_copy(q_hbm.at[0], qv, ld_w.at[0])
    pa_load = pltpu.make_async_copy(pa_hbm, pav, ld_w.at[1])
    pe_load = pltpu.make_async_copy(pe_hbm, pev, ld_w.at[2])
    q_load.start()
    pa_load.start()
    pe_load.start()
    for h in range(2):
        act_load(h).start()
        err_load(h).start()

    barrier = pltpu.get_barrier_semaphore()

    def signal(dev):
        pl.semaphore_signal(barrier, inc=1, device_id=dev, device_id_type=MESH)

    each(1, NW, lambda d: signal((lax.rem(w + d, NW), q)))
    each(1, NQ, lambda d: signal((w, lax.rem(q + d, NQ))))
    hold_w, hold_q = q // 2, core * 8 + w
    from_w, from_q = lax.rem(q, 8), 2 * w + q // 8
    keeps = jnp.logical_and(hold_w == w, hold_q == q)
    moves = jnp.logical_not(keeps)

    @pl.when(moves)
    def _():
        signal((hold_w, hold_q))
        signal((from_w, from_q))

    q_load.wait()
    step_one = qv[...] / center
    vsrc[...] = step_one.T.astype(BF16)

    def cols(block):
        return (slice(None), ds(block * BLK, BLK, BLK))

    zq = qpeer(8)

    def y_peer(d):
        return q // 8 * 8 + lax.rem(q + 2 * d, 8)

    def over(i):
        return lax.rem(i + 8, NQ)

    def tile(view, some, ssem, rsem, y_first=False):
        def hand(i):
            send(view(i), view(i), ssem + 1, rsem + 3, (w, sib))

        def along_y():
            each(1, 4, lambda d: send(view(q), view(q), ssem, rsem + 1, (w, y_peer(d))))

        def along_z():
            send(view(q), view(q), ssem, rsem, (w, zq))

        def start():
            (along_y if y_first else along_z)()

        def rest():
            (along_z if y_first else along_y)()
            hand(q)

        def relay():
            if y_first:
                took(some(3), rsem + 1)

                def step(d):
                    i = y_peer(d)
                    send(view(i), view(i), ssem, rsem + 2, (w, zq))
                    hand(i)

                each(1, 4, step)
            else:
                took(some(1), rsem)
                each(1, 4, lambda d: send(view(zq), view(zq), ssem, rsem + 2, (w, y_peer(d))))
                hand(zq)

        def forward():
            if y_first:
                took(some(1), rsem)
                hand(zq)
            else:
                took(some(3), rsem + 1)
                each(1, 4, lambda d: hand(y_peer(d)))
            took(some(3), rsem + 2)
            each(1, 4, lambda d: hand(over(y_peer(d))))

        def done():
            took(some(8), rsem + 3)

        def drain():
            left(some(7), ssem)
            left(some(8), ssem + 1)

        return start, rest, relay, forward, done, drain

    def halves(first, second):
        def both(pair_of):
            def run():
                for f in pair_of:
                    f()

            return run

        return [both(pair_of) for pair_of in zip(first, second)]

    def pc_half(r):
        return (lambda i: pc.at[r * 64:(r + 1) * 64, ds(i * BLK, BLK, BLK)], lambda n: pc.at[0:64, 0:n * BLK])

    def panel_half(r):
        return (
            lambda i: panel.at[ds(i * 16, 16, 16), r * 1024:(r + 1) * 1024],
            lambda n: panel.at[0:n * 16, 0:1024],
        )

    v_start, v_rest, v_relay, v_forward, v_done, v_drain = tile(lambda i: vc.at[cols(i)], lambda n: vc.at[:, 0:n * BLK], S_VT, R_VT)
    p_start, p_rest, p_relay, p_forward, p_done, p_drain = halves(
        tile(*pc_half(0), S_P, R_P), tile(*pc_half(1), S_PB, R_PB, True)
    )
    g_start, g_rest, g_relay, g_forward, g_done, g_drain = halves(
        tile(*panel_half(0), S_G, R_G), tile(*panel_half(1), S_GB, R_GB, True)
    )

    zw = wpeer(4)

    def x_peer(d):
        return zl * 4 + lax.rem(xw + d, 4)

    def project(h):
        rows = load_rows(h)
        pa[rows, :] = mm(actv[rows, :], pav[...], NN)
        pe[rows, :] = mm(errv[rows, :], pev[...], NN)

    def token_rows(block):
        return ds(block * BLK, BLK, BLK)

    def project_send(h):
        if h < 2:
            send(pa.at[load_rows(h), :], ra.at[h * 256:(h + 1) * 256, :], S_PJ, (R_PJ, R_PJB)[h], (zw, q))
        half = lax.rem(1 - zl + h // 2, 2)

        def step(d):
            x = h % 2 * 2 + lax.rem(xw + d, 2)

            @pl.when(x != xw)
            def _():
                send(pe.at[token_rows(half * 4 + x), :], re.at[xw, half], S_PE, (R_PE, R_PEB)[h // 2], (zl * 4 + x, q))

        each(0, 2, step)

    def project_act(h):
        took(ra.at[0:256, :], (R_PJ, R_PJB)[h])

        def step(d):
            x = h * 2 + lax.rem(xw + d, 2)
            sa[x] = pa[token_rows(zl * 4 + x), :] + ra[token_rows(x), :]

            @pl.when(x != xw)
            def _():
                send(sa.at[x], ra2.at[xw], S_PA2, R_PA2, (zl * 4 + x, q))

        each(0, 2, step)

    def err_half(half):
        total = pe[token_rows(half * 4 + xw), :]
        for d in range(1, 4):
            total = total + re[lax.rem(xw + d, 4), half]
        return total

    def project_err():
        took(re.at[0:3, 0], R_PE)
        se[...] = err_half(1 - zl)
        send(se, re2, S_PE2, R_PE2, (zw, q))

    def project_total():
        took(re.at[0:3, 0], R_PEB)
        err = err_half(zl)
        took(re2, R_PE2)
        err = err + re2[...]
        took(ra2.at[0:3], R_PA2)
        act = sa[xw]
        for d in range(1, 4):
            act = act + ra2[lax.rem(xw + d, 4)]
        return act, err

    def load_wait(h):
        act_load(h).wait()
        err_load(h).wait()

    pa_load.wait()
    pe_load.wait()
    load_wait(0)
    for h in (2, 3):
        act_load(h).start()
        err_load(h).start()
    project(0)

    pl.semaphore_wait(barrier, (NW - 1) + (NQ - 1) + 2 * moves.astype(jnp.int32))

    vr[cols(w)] = vsrc[...]
    each(1, NW, lambda d: send(vsrc, vr.at[cols(w)], S_V, R_V, (wpeer(d), q)))

    @pl.when(moves)
    def _():
        send(vsrc, vc.at[cols(hold_q)], S_HV, R_HV, (hold_w, hold_q))

    @pl.when(keeps)
    def _():
        vc[cols(q)] = vsrc[...]

    project_send(0)
    load_wait(1)
    project(1)
    project_send(1)
    load_wait(2)
    for j in range(4):
        f_load(j).start()
    project(2)
    project_send(2)
    load_wait(3)
    project(3)
    project_send(3)

    def cast_f(j):
        @pl.when(lax.rem(j, 2) == 0)
        def _():
            f_load(j // 2).wait()

        rows = ds(j * BLK, BLK, BLK)
        fb[rows, :] = fv[rows, :].astype(BF16)

        @pl.when(diag)
        def _():
            mid = ds(core * 1024 + j * BLK, BLK, BLK)
            eye = lax.broadcasted_iota(jnp.int32, (BLK, BLK), 0) == lax.broadcasted_iota(jnp.int32, (BLK, BLK), 1)
            fb[rows, mid] = (fv[rows, mid] - jnp.where(eye, center, 0.0)).astype(BF16)

    each(0, 8, cast_f)

    def width_sum(own, recv):
        total = own
        for d in range(1, NW):
            total = total + recv[wpeer(d)].astype(F32)
        return total

    took(vr.at[:, 0:7 * BLK], R_V)

    def apply_transposed(m):
        both = mm(vr[...], fb[:, ds(m * 256, 256, 256)], NN)
        even, odd = both[:, 0:128], both[:, 128:256]
        first = core == 0
        ykeep[m] = jnp.where(first, even, odd)
        ygive[m] = jnp.where(first, odd, even).astype(BF16)

    each(0, 8, apply_transposed)
    send(ygive, ytake, S_GIVE, R_GIVE, (w, sib))
    @pl.when(moves)
    def _():
        took(vc.at[cols(q)], R_HV)

    v_start()
    v_rest()
    project_act(0)
    project_err()
    project_act(1)
    took(ytake, R_GIVE)

    def y_send(d):
        m = lax.rem(pair + d, 8)
        ysend[m] = (ykeep[m] + ytake[m].astype(F32)).astype(BF16)
        send(ysend.at[m], yrecv.at[pair], S_Y, R_Y, (w, 2 * m + core))

    each(1, 8, y_send)

    v_relay()
    own_rows = ds(w * BLK, BLK, BLK)
    act_sum, err_sum = project_total()
    for s in range(2):
        act = act_sum[s * SEQ_LEN:(s + 1) * SEQ_LEN, :]
        err = err_sum[s * SEQ_LEN:(s + 1) * SEQ_LEN, :]
        grad = lax.dot_general(
            err.T, act, NN, precision=lax.Precision.HIGHEST, preferred_element_type=F32
        )
        gown[s] = (grad / SEQ_LEN).astype(BF16)

    for i in far_w:
        send(gown.at[:, ds(i * 16, 16, 16), :], dbuf.at[pl.ds(2 * w, 2)], S_D, R_D, (i, q))

    dbuf[pl.ds(2 * w, 2)] = gown[:, ds(w * 16, 16, 16), :]

    took(yrecv.at[0:7], R_Y)
    y_block = ykeep[pair] + ytake[pair].astype(F32)
    for d in range(1, 8):
        y_block = y_block + yrecv[lax.rem(pair + d, 8)].astype(F32)
    yback[...] = y_block
    pc[cols(q)] = (-y_block - ridge_damp * vc[cols(q)].astype(F32)).astype(BF16)
    p_start()
    p_rest()

    @pl.when(moves)
    def _():
        send(yback, yown, S_HY, R_HY, (from_w, from_q))

    @pl.when(keeps)
    def _():
        yown[...] = y_block

    v_forward()
    took(dbuf.at[0:14], R_D)
    dwide[...] = dbuf[...].astype(F32)
    seq_rows = ds(q * 16, 16, 16)
    for i in range(16):
        panel[seq_rows, i * BLK:(i + 1) * BLK] = dwide[:, i, :].astype(BF16)

    g_start()
    g_rest()

    def seq_products(value, out, part, ssem, rsem):
        out[...] = value
        part[w] = value
        for i in far_w:
            send(out, part.at[w], ssem, rsem, (i, q))

    def seq_gather(part, whole, rsem, asem, arsem):
        took(part.at[0:7], rsem)
        total = part[0]
        for i in range(1, NW):
            total = total + part[i]
        whole[seq_rows, :] = total.astype(BF16)
        mine = whole.at[seq_rows, :]
        for i in far_q:
            send(mine, mine, asem, arsem, (w, i))
        return total

    v_done()
    seq_products(mm(panel[seq_rows, :], vc[...], NT), t1send, t1part, S_T1, R_T1)
    p_relay()
    g_relay()
    t1sum[...] = seq_gather(t1part, t1all, R_T1, S_T1A, R_T1A)
    p_forward()
    g_forward()
    p_done()
    gpart = mm(panel[seq_rows, :], pc[...], NT)
    g_done()

    @pl.when(moves)
    def _():
        send(panel.at[:, ds(q * BLK, BLK, BLK)], gmine, S_GO, R_GO, (from_w, from_q))

    @pl.when(keeps)
    def _():
        gmine[...] = panel[:, ds(q * BLK, BLK, BLK)]

    kpart = mm(panel[seq_rows, :], panel[...], NT).astype(BF16)
    took(t1all.at[0:240, :], R_T1A)
    t1b = t1all[...]
    seq_products(gpart - mm(kpart, t1b, NN) / SEQS, t2send, t2part, S_T2, R_T2)
    for k in range(4):
        part = slice(k * 512, (k + 1) * 512)
        wt = mm(t1b, panel[:, part], TN)
        rt[:, part] = (pc[:, part].astype(F32) - wt / SEQS).astype(BF16)

    def apply_rows(j):
        rows = ds(j * 512, 512, 512)
        zsend[rows, :] = mm(fb[rows, :], rt[...], NT).astype(BF16)

    each(0, 2, apply_rows)
    each(1, NW, lambda d: send(zsend.at[ds(wpeer(d) * BLK, BLK, BLK), :], zrecv.at[w], S_Z, R_Z, (wpeer(d), q)))
    t2sum = seq_gather(t2part, t2all, R_T2, S_T2A, R_T2A)
    score[...] = (1.0 + coef_one) * t1sum[...] + coef_res * t2sum

    @pl.when(moves)
    def _():
        send(score, smine, S_SC, R_SC, (hold_w, hold_q))

    @pl.when(keeps)
    def _():
        smine[...] = score[...]

    @pl.when(moves)
    def _():
        took(gmine, R_GO)
        took(yown, R_HY)

    one = qv[...] / center
    y_shift = yown[...].T
    w_own = mm(gmine[...], t1b, TN) / SEQS
    res_one = -y_shift - ridge_damp * one - w_own
    step_two = coef_one * one + coef_res * res_one
    sol_ref[0] = one + step_two

    left(vr.at[:, 0:7 * BLK], S_V)
    left(ra, S_PJ)
    left(re.at[0:3], S_PE)
    left(ra2.at[0:3], S_PA2)
    left(re2, S_PE2)
    v_drain()
    left(ygive, S_GIVE)
    left(ysend.at[0:7], S_Y)
    left(dbuf.at[0:14], S_D)
    p_drain()
    g_drain()
    left(t1part.at[0:7], S_T1)
    left(t1all.at[0:240, :], S_T1A)
    left(t2part.at[0:7], S_T2)

    @pl.when(moves)
    def _():
        left(vsrc, S_HV)
        left(yback, S_HY)
        left(gmine, S_GO)

    took(zrecv.at[0:7], R_Z)
    z_own = center * res_one + width_sum(zsend[own_rows, :].astype(F32), zrecv)
    f_two = coef_one * (center * one + y_shift) + coef_res * z_own
    base = res_one - f_two - ridge_damp * step_two - coef_one * w_own

    took(t2all.at[0:240, :], R_T2A)
    g_two = mm(gmine[...], t2all[...], TN) / SEQS
    res_ref[0] = base - coef_res * g_two

    @pl.when(moves)
    def _():
        took(score, R_SC)
        left(score, S_SC)

    sc_ref[...] = smine[pl.ds(2 * from_w, 2), :]
    left(zrecv.at[0:7], S_Z)
    left(t2all.at[0:240, :], S_T2A)


def settle(sol_in, res_in, sc_in, sol_ref, res_ref, sc_ref, sems):
    copies = [
        pltpu.make_async_copy(src, dst, sems.at[i])
        for i, (src, dst) in enumerate(((sol_in, sol_ref), (res_in, res_ref), (sc_in, sc_ref)))
    ]
    for copy in copies:
        copy.start()
    for copy in copies:
        copy.wait()


def on_device(activations, errors, proj_acts, proj_errs, fisher, queries):
    vm = pltpu.VMEM
    dma = pltpu.SemaphoreType.DMA
    scratch = [
        vm((1024, 3584), BF16), vm((1024, 1024), BF16), vm((3584, 128), BF16), vm((1024, 128), BF16),
        vm((1024, 2048), F32), vm((1024, 2048), BF16), vm((128, 128), F32),
        vm((1024, 128), F32), vm((1024, 128), F32), vm((512, 128), F32), vm((4, 2, 128, 128), F32),
        vm((4, 128, 128), F32), vm((128, 128), F32), vm((4, 128, 128), F32), vm((128, 128), F32),
        vm((128, 128), BF16), vm((128, 1024), BF16), vm((128, 2048), BF16), vm((128, 2048), BF16), vm((128, 2048), BF16),
        vm((8, 128, 128), F32), vm((8, 128, 128), BF16), vm((8, 128, 128), BF16), vm((8, 128, 128), BF16),
        vm((8, 128, 128), BF16), vm((128, 128), F32), vm((128, 128), F32), vm((1024, 128), BF16), vm((8, 128, 128), BF16),
        vm((2, 128, 128), BF16), vm((16, 16, 128), BF16), vm((16, 16, 128), F32), vm((256, 2048), BF16), vm((256, 128), BF16),
        vm((16, 128), F32), vm((8, 16, 128), F32), vm((16, 128), F32), vm((256, 128), BF16),
        vm((16, 128), F32), vm((8, 16, 128), F32), vm((256, 128), BF16), vm((16, 128), F32), vm((16, 128), F32),
        dma((4,)), dma((4,)), dma((3,)), dma((4,)), dma((27,)), dma((39,)),
    ]
    hbm = pl.BlockSpec(memory_space=pl.ANY)
    operands = (activations, errors, proj_acts, proj_errs, fisher, queries)
    vmem = pl.BlockSpec(memory_space=pltpu.VMEM)
    raw = pl.pallas_call(
        kernel,
        out_shape=(
            jax.ShapeDtypeStruct((1, 128, 128), F32),
            jax.ShapeDtypeStruct((1, 128, 128), F32),
            jax.ShapeDtypeStruct((2, 128), F32),
        ),
        in_specs=[hbm] * 6,
        out_specs=(vmem, vmem, vmem),
        scratch_shapes=scratch,
        compiler_params=pltpu.CompilerParams(
            collective_id=0, has_side_effects=True, vmem_limit_bytes=34 * 1024 * 1024
        ),
    )(*[pltpu.with_memory_space_constraint(a, pltpu.HBM) for a in operands])
    return pl.pallas_call(
        settle,
        out_shape=tuple(jax.ShapeDtypeStruct(r.shape, r.dtype) for r in raw),
        in_specs=[hbm] * 3,
        out_specs=(hbm, hbm, hbm),
        scratch_shapes=[dma((3,))],
        compiler_params=pltpu.CompilerParams(vmem_limit_bytes=4 * 1024 * 1024),
    )(*raw)


def solution(mesh):
    placed = (
        P("seq", "width"),
        P("seq", "width"),
        P("width", None),
        P("width", None),
        P("seq", "width"),
        P("seq", "width", None),
    )
    return jax.shard_map(
        on_device,
        mesh=mesh,
        in_specs=placed,
        out_specs=(P("seq", "width", None), P("seq", "width", None), P(("width", "seq"), None)),
        check_vma=False,
    )
```
